128 devices in a mesh: curves: 32 (over x, y_lo, z), tm: 4 (over y_hi, core).
Axes of the slice: x: 4, y: 4 (y_hi: 2, y_lo: 2; y = y_hi * 2 + y_lo), z: 4, core: 2. Of those that a mesh axis runs over, the one named last changes fastest.
Arguments:
- curves_data: float32 [24576, 16384], P('curves', 'tm'), as said below
- loadings: float32 [24576, 256], P('curves'), may hold values from 0 to 10, as said below
- profiles: float32 [16384, 256], P('tm'), may hold values from 0 to 5, as said below
- counts: int32 [32], replicated, may hold values from 1 to 768, as said below
Outputs:
- new_loadings: float32 [24576, 256], P('curves')
- new_profiles: float32 [16384, 256], P('tm')
The draws below stay inside these ranges and needn't reach their ends.
Inputs may be any that keep to these rules, and one draw needn't show every extreme that they name: counts[i] curves of campaign i fill the first slots of its 768; for i < 16, the blocks of 128 slots that campaigns i and i + 16 occupy (each rounded up) total at most 8; some campaign fills all its slots. `loadings`: nonnegative. `profiles`: nonnegative. `curves_data`: nonnegative.
All inputs are finite; a program needn't handle non-finite values.
Results may differ from the reference program's by a relative error of at most 0.00025.
Values sent between devices are 32-bit elements; how exact they have to be, the bound alone decides.
No kernel may reach another device: no remote copies, remote signals or barrier semaphores. Data moves between devices by JAX's collectives and lax.ppermute only.
A program may use at most 128 MiB of HBM per device.

```python
import math
import jax
import jax.numpy as jnp
from jax import lax

COMPS = 256
TPTS = 16384
BLOCK = 128
MAXBLK = 6
PAIRBLK = 4
ROWS = 768
CURVES_ALL = 24576
N_CURVES = 32


def make_loadings(key):
    first, second = jax.random.split(jax.random.fold_in(key, 11), 2)
    base = jnp.exp(jax.random.uniform(first, (CURVES_ALL, COMPS), jnp.float32, math.log(0.05), math.log(0.5)))
    column = jnp.exp(jax.random.uniform(second, (1, COMPS), jnp.float32, math.log(0.5), math.log(2.0)))
    where_at = jnp.arange(CURVES_ALL, dtype=jnp.float32) / CURVES_ALL
    rising = 1.0 + 2.0 * where_at
    return (base * column * rising[:, None]).astype(jnp.float32)


def make_profiles(key):
    first, second, third = jax.random.split(jax.random.fold_in(key, 12), 3)
    base = jnp.exp(jax.random.uniform(first, (TPTS, COMPS), jnp.float32, math.log(0.05), math.log(0.5)))
    column = jnp.exp(jax.random.uniform(second, (1, COMPS), jnp.float32, math.log(0.3), math.log(3.0)))
    scale_rows = jnp.exp(jax.random.uniform(third, (TPTS,), jnp.float32, math.log(0.3), math.log(3.0)))
    return (base * column * scale_rows[:, None]).astype(jnp.float32)


def draw_loadings(key, part):
    return make_loadings(key)


def draw_profiles(key, part):
    return make_profiles(key)


def draw_curves_data(key, part):
    fitted = jnp.dot(make_loadings(key), make_profiles(key).T, precision=lax.Precision.HIGHEST)
    noise_key = jax.random.fold_in(key, 13)
    noise = 0.4 * jax.random.uniform(noise_key, (CURVES_ALL, TPTS), jnp.float32, -1.0, 1.0)
    return (fitted * (1.0 + noise)).astype(jnp.float32)


def draw_counts(key, part):
    half = N_CURVES // 2
    key_heavy, key_light, key_side, key_pick = jax.random.split(jax.random.fold_in(key, 14), 4)
    heavy = jax.random.randint(key_heavy, (half,), 1, ROWS + 1)
    forced = jax.random.randint(key_pick, (), 0, half)
    heavy = jnp.where(jnp.arange(half) == forced, ROWS, heavy)
    heavy_blocks = (heavy + BLOCK - 1) // BLOCK
    room = jnp.minimum(2 * PAIRBLK - heavy_blocks, MAXBLK) * BLOCK
    light = jax.random.randint(key_light, (half,), 1, room + 1)
    side = jax.random.randint(key_side, (half,), 0, 2)
    first = jnp.where(side == 1, heavy, light)
    second = jnp.where(side == 1, light, heavy)
    return jnp.concatenate([first, second]).astype(jnp.int32)


def setup_inputs(seed: int = 0) -> dict:
    arg_keys = jax.random.split(jax.random.key(seed), 5)
    curves_data = draw_curves_data(jax.random.fold_in(arg_keys[4], 71), 0)
    loadings = draw_loadings(jax.random.fold_in(arg_keys[4], 71), 0)
    profiles = draw_profiles(jax.random.fold_in(arg_keys[4], 71), 0)
    counts = draw_counts(jax.random.fold_in(arg_keys[4], 71), 0)
    return dict(curves_data=curves_data, loadings=loadings, profiles=profiles, counts=counts)


def reference(curves_data, loadings, profiles, counts):
    high = lax.Precision.HIGHEST
    data = curves_data.reshape(N_CURVES, ROWS, TPTS)
    load = loadings.reshape(N_CURVES, ROWS, COMPS)
    live = lax.iota(jnp.int32, ROWS)[None, :] < counts[:, None]

    def campaign(total, item):
        block, weights, alive = item
        recon = jnp.dot(weights, profiles.T, precision=high)
        resid = jnp.where(alive[:, None], block - recon, 0.0)
        row_grad = jnp.dot(resid, profiles, precision=high)
        total = total + jnp.dot(resid.T, weights, precision=high)
        return total, row_grad

    time_grad, row_grad = lax.scan(campaign, jnp.zeros((TPTS, COMPS), jnp.float32), (data, load, live))
    row_grad = row_grad.reshape(N_CURVES * ROWS, COMPS)
    alive = live.reshape(N_CURVES * ROWS)[:, None]
    time_norm = jnp.sum(profiles * profiles, axis=0)
    curve_norm = jnp.sum(jnp.where(alive, loadings * loadings, 0.0), axis=0)
    new_loadings = jnp.where(alive, jnp.maximum(loadings + row_grad / time_norm, 0.0), 0.0)
    new_profiles = jnp.maximum(profiles + time_grad / curve_norm, 0.0)
    return new_loadings, new_profiles
```

```python
import functools

import jax
import jax.numpy as jnp
from jax import lax
from jax.experimental import pallas as pl
from jax.experimental.pallas import tpu as pltpu
from jax.sharding import PartitionSpec as P


ROWS = 768
COMPS = 256
POINTS = 4096
COLOUR = POINTS // 2
TILE = 256
PIECE = COLOUR // 16
HALF = ROWS // 2
PAD = 8
F32 = jnp.float32
BF16 = jnp.bfloat16

ORDER = {(0, 0): (0, 1, 2, 3), (0, 1): (1, 0, 3, 2), (1, 0): (2, 3, 0, 1), (1, 1): (3, 2, 1, 0)}


def flip(bit, x, z):
    if bit == 0:
        return x ^ 1, z
    if bit == 1:
        return 3 - x, z
    if bit == 2:
        return x, z ^ 1
    return x, 3 - z


def pairs(move):
    out = []
    for x in range(4):
        for y in range(2):
            for z in range(4):
                for hi in range(2):
                    for core in range(2):
                        tx, ty, tz, thi, tcore = move(x, y, z, hi, core)
                        source = (x * 8 + y * 4 + z) * 4 + hi * 2 + core
                        target = (tx * 8 + ty * 4 + tz) * 4 + thi * 2 + tcore
                        out.append((source, target))
    return out


def cube_pairs(colour, step):
    def move(x, y, z, hi, core):
        tx, tz = flip(ORDER[core, colour][step], x, z)
        return tx, y, tz, hi, core

    return pairs(move)


Y_PAIRS = pairs(lambda x, y, z, hi, core: (x, 1 - y, z, hi, core))
HI_PAIRS = pairs(lambda x, y, z, hi, core: (x, y, z, 1 - hi, core))
CORE_PAIRS = pairs(lambda x, y, z, hi, core: (x, y, z, hi, 1 - core))


def swap(value, table):
    return lax.ppermute(value, ("curves", "tm"), table)


def my_label():
    index = lax.axis_index("curves")
    x, z = index // 8, index % 4
    return (x ^ (x >> 1)) | ((z ^ (z >> 1)) << 2)


def my_core():
    return lax.axis_index("tm") % 2


def arranged(bits, colour):
    one = [(bits >> i) & 1 for i in range(4)]
    views = []
    for core in range(2):
        order = ORDER[core, colour]
        views.append(sum(one[order[3 - i]] << i for i in range(4)))
    return jnp.where(my_core() == 0, views[0], views[1])


def placed(position, colour):
    one = [(position >> i) & 1 for i in range(4)]
    views = []
    for core in range(2):
        order = ORDER[core, colour]
        views.append(sum(one[3 - i] << order[i] for i in range(4)))
    return jnp.where(my_core() == 0, views[0], views[1])


def split(value):
    high = value.astype(BF16)
    return high, (value - high.astype(F32)).astype(BF16)


def dot(a, b):
    return jnp.dot(a, b, preferred_element_type=F32)


def time_kernel(colour, counts, data, load, prof, send, keep, own, wide, gram_high, gram_low):
    step = pl.program_id(0)
    label = my_label()

    @pl.when(step == 0)
    def _():
        live = counts[lax.axis_index("curves")]
        alive = lax.broadcasted_iota(jnp.int32, (ROWS, COMPS), 0) < live
        weights = jnp.where(alive, load[...], 0.0)
        high, low = split(weights)
        high_t, low_t = high.T, low.T
        wide[:COMPS] = high_t
        wide[COMPS:] = low_t
        gram = dot(high_t, high) + dot(high_t, low) + dot(low_t, high)
        gram_high[...], gram_low[...] = split(gram)
        norm = jnp.sum(weights * weights, axis=0, keepdims=True)
        norm = jnp.broadcast_to(norm, (PAD, COMPS))
        send[8 * PIECE :] = norm
        keep[8 * PIECE :] = norm

    high, low = split(data[...])
    both = dot(wide[...], high)
    back = both[:COMPS] + both[COMPS:] + dot(wide[:COMPS], low)
    points = prof[...]
    phigh, plow = split(points)
    fitted = dot(phigh, gram_high[...]) + dot(plow, gram_high[...]) + dot(phigh, gram_low[...])
    grad = back.T - fitted
    for part in range(TILE // PIECE):
        piece = step * (TILE // PIECE) + part
        rows = grad[part * PIECE : (part + 1) * PIECE]
        position = arranged(piece ^ label, colour)
        start = pl.multiple_of((position & 7) * PIECE, PIECE)

        @pl.when(position >= 8)
        def _():
            send[pl.ds(start, PIECE)] = rows

        @pl.when(position < 8)
        def _():
            keep[pl.ds(start, PIECE)] = rows

        @pl.when(piece == label)
        def _():
            own[...] = points[part * PIECE : (part + 1) * PIECE]


def time_part(colour, counts, data, load, prof):
    steps = COLOUR // TILE
    base = colour * steps
    message = jax.ShapeDtypeStruct((8 * PIECE + PAD, COMPS), F32)
    whole = pl.BlockSpec((8 * PIECE + PAD, COMPS), lambda i, c: (0, 0))
    return pl.pallas_call(
        functools.partial(time_kernel, colour),
        out_shape=(message, message, jax.ShapeDtypeStruct((PIECE, COMPS), F32)),
        grid_spec=pltpu.PrefetchScalarGridSpec(
            num_scalar_prefetch=1,
            grid=(steps,),
            in_specs=[
                pl.BlockSpec((ROWS, TILE), lambda i, c: (0, base + i)),
                pl.BlockSpec((ROWS, COMPS), lambda i, c: (0, 0)),
                pl.BlockSpec((TILE, COMPS), lambda i, c: (base + i, 0)),
            ],
            out_specs=(whole, whole, pl.BlockSpec((PIECE, COMPS), lambda i, c: (0, 0))),
            scratch_shapes=[
                pltpu.VMEM((2 * COMPS, ROWS), BF16),
                pltpu.VMEM((COMPS, COMPS), BF16),
                pltpu.VMEM((COMPS, COMPS), BF16),
            ],
        ),
        cost_estimate=pl.CostEstimate(
            flops=6 * COLOUR * COMPS * (ROWS + COMPS), bytes_accessed=4 * COLOUR * (ROWS + 2 * COMPS), transcendentals=0
        ),
        name=f"time_part{colour}",
    )(counts, data, load, prof)


def row_kernel(counts, data, load, prof, send, keep, base, total, square, cross, norm):
    step = pl.program_id(0)

    @pl.when(step == 0)
    def _():
        total[...] = jnp.zeros_like(total)
        square[...] = jnp.zeros_like(square)
        cross[...] = jnp.zeros_like(cross)
        norm[...] = jnp.zeros_like(norm)

    high, low = split(data[...])
    points = prof[...]
    phigh, plow = split(points)
    total[...] += dot(high, phigh) + dot(low, phigh) + dot(high, plow)
    phigh_t = phigh.T
    square[...] += dot(phigh_t, phigh)
    cross[...] += dot(phigh_t, plow)
    norm[...] += jnp.broadcast_to(jnp.sum(points * points, axis=0, keepdims=True), norm.shape)

    @pl.when(step == pl.num_programs(0) - 1)
    def _():
        mixed = cross[...]
        gram = square[...] + mixed + mixed.T
        total[...] -= jnp.dot(load[...], gram, precision=lax.Precision.HIGHEST, preferred_element_type=F32)
        mine = pl.multiple_of(my_core() * HALF, HALF)
        other = pl.multiple_of(HALF - my_core() * HALF, HALF)
        send[:HALF] = total[pl.ds(other, HALF)]
        keep[:HALF] = total[pl.ds(mine, HALF)]
        send[HALF:] = norm[...]
        keep[HALF:] = norm[...]
        base[...] = load[pl.ds(mine, HALF)]


def row_part(counts, data, load, prof):
    message = jax.ShapeDtypeStruct((HALF + PAD, COMPS), F32)
    whole = pl.BlockSpec((HALF + PAD, COMPS), lambda i, c: (0, 0))
    return pl.pallas_call(
        row_kernel,
        out_shape=(message, message, jax.ShapeDtypeStruct((HALF, COMPS), F32)),
        grid_spec=pltpu.PrefetchScalarGridSpec(
            num_scalar_prefetch=1,
            grid=(POINTS // TILE,),
            in_specs=[
                pl.BlockSpec((ROWS, TILE), lambda i, c: (0, i)),
                pl.BlockSpec((ROWS, COMPS), lambda i, c: (0, 0)),
                pl.BlockSpec((TILE, COMPS), lambda i, c: (i, 0)),
            ],
            out_specs=(whole, whole, pl.BlockSpec((HALF, COMPS), lambda i, c: (0, 0))),
            scratch_shapes=[
                pltpu.VMEM((ROWS, COMPS), F32),
                pltpu.VMEM((COMPS, COMPS), F32),
                pltpu.VMEM((COMPS, COMPS), F32),
                pltpu.VMEM((PAD, COMPS), F32),
            ],
        ),
        cost_estimate=pl.CostEstimate(
            flops=6 * POINTS * COMPS * (ROWS + COMPS), bytes_accessed=4 * POINTS * (ROWS + COMPS), transcendentals=0
        ),
        name="row_part",
    )(counts, data, load, prof)


def gather_kernel(count, *refs):
    out = refs[-1]
    rows = out.shape[0] - PAD
    out[:rows] = functools.reduce(lambda a, b: a + b, [r[...] for r in refs[:count]])
    out[rows:] = functools.reduce(lambda a, b: a + b, [r[...] for r in refs[count : 2 * count]])


def merged(messages, rows, index):
    count = len(messages)
    specs = [pl.BlockSpec((rows, COMPS), lambda g, i=index: (i, 0)) for _ in messages]
    specs += [pl.BlockSpec((PAD, COMPS), lambda g, i=m.shape[0] // PAD - 1: (i, 0)) for m in messages]
    return pl.pallas_call(
        functools.partial(gather_kernel, count),
        out_shape=jax.ShapeDtypeStruct((rows + PAD, COMPS), F32),
        grid=(1,),
        in_specs=specs,
        out_specs=pl.BlockSpec((rows + PAD, COMPS), lambda g: (0, 0)),
        cost_estimate=pl.CostEstimate(
            flops=rows * COMPS * count, bytes_accessed=4 * rows * COMPS * (count + 1), transcendentals=0
        ),
        name="merged",
    )(*messages, *messages)


def update_kernel(base, mine, other, out):
    rows = out.shape[0]
    grad = mine[:rows] + other[:rows]
    norm = mine[rows : rows + 1] + other[rows : rows + 1]
    out[...] = jnp.maximum(base[...] + grad / norm, 0.0)


def updated(base, mine, other):
    return pl.pallas_call(
        update_kernel,
        out_shape=jax.ShapeDtypeStruct(base.shape, F32),
        cost_estimate=pl.CostEstimate(flops=4 * base.size, bytes_accessed=16 * base.size, transcendentals=0),
        name="updated",
    )(base, mine, other)


def load_kernel(counts, base, mine, other, out):
    rows = out.shape[0]
    grad = mine[:rows] + other[:rows]
    norm = mine[rows : rows + 1] + other[rows : rows + 1]
    fresh = jnp.maximum(base[...] + grad / norm, 0.0)
    slot = lax.broadcasted_iota(jnp.int32, fresh.shape, 0) + my_core() * HALF
    out[...] = jnp.where(slot < counts[lax.axis_index("curves")], fresh, 0.0)


def load_update(counts, base, mine, other):
    vmem = pl.BlockSpec(memory_space=pltpu.VMEM)
    return pl.pallas_call(
        load_kernel,
        out_shape=jax.ShapeDtypeStruct(base.shape, F32),
        in_specs=[pl.BlockSpec(memory_space=pltpu.SMEM), vmem, vmem, vmem],
        cost_estimate=pl.CostEstimate(flops=4 * base.size, bytes_accessed=16 * base.size, transcendentals=0),
        name="load_update",
    )(counts, base, mine, other)


def join_kernel(mine, other, out, sems):
    core = my_core()
    first = pltpu.make_async_copy(mine, out.at[pl.ds(pl.multiple_of(core * HALF, HALF), HALF)], sems.at[0])
    second = pltpu.make_async_copy(other, out.at[pl.ds(pl.multiple_of(HALF - core * HALF, HALF), HALF)], sems.at[1])
    first.start()
    second.start()
    first.wait()
    second.wait()


def joined(mine, other):
    vmem = pl.BlockSpec(memory_space=pltpu.VMEM)
    return pl.pallas_call(
        join_kernel,
        out_shape=jax.ShapeDtypeStruct((ROWS, COMPS), F32),
        in_specs=[vmem, vmem],
        out_specs=pl.BlockSpec(memory_space=pl.ANY),
        scratch_shapes=[pltpu.SemaphoreType.DMA((2,))],
        name="joined",
    )(mine, other)


def store_kernel(first, *refs):
    left, right = refs[0], refs[1]
    out, sems = refs[-2], refs[-1]
    label = my_label()
    copies = []
    for colour, source in enumerate((left, right)):
        for i in range(8):
            piece = placed(first + i, colour) ^ label
            start = pl.multiple_of(colour * COLOUR + piece * PIECE, PIECE)
            copies.append(
                pltpu.make_async_copy(
                    source.at[pl.ds(i * PIECE, PIECE)], out.at[pl.ds(start, PIECE)], sems.at[colour * 8 + i]
                )
            )
    for copy in copies:
        copy.start()
    for copy in copies:
        copy.wait()


def stored(first, left, right, held=None):
    vmem = pl.BlockSpec(memory_space=pltpu.VMEM)
    args, specs, alias = [left, right], [vmem, vmem], {}
    if held is not None:
        args.append(held)
        specs.append(pl.BlockSpec(memory_space=pl.ANY))
        alias = {2: 0}
    return pl.pallas_call(
        functools.partial(store_kernel, first),
        out_shape=jax.ShapeDtypeStruct((POINTS, COMPS), F32),
        in_specs=specs,
        out_specs=pl.BlockSpec(memory_space=pl.ANY),
        scratch_shapes=[pltpu.SemaphoreType.DMA((16,))],
        input_output_aliases=alias,
        cost_estimate=pl.CostEstimate(flops=0, bytes_accessed=16 * left.size, transcendentals=0),
        name="stored",
    )(*args)


def local(curves_data, loadings, profiles, counts):
    messages, owns = [], []
    for colour in range(2):
        send, keep, own = time_part(colour, counts, curves_data, loadings, profiles)
        messages.append([keep, swap(send, cube_pairs(colour, 0))])
        owns.append(own)
    row_send, row_keep, row_base = row_part(counts, curves_data, loadings, profiles)
    row_other = swap(row_send, CORE_PAIRS)

    rows = 4 * PIECE
    for step in range(1, 4):
        for colour in range(2):
            send = merged(messages[colour], rows, 1)
            messages[colour].append(swap(send, cube_pairs(colour, step)))
        rows //= 2
    fresh = []
    for colour in range(2):
        mine = merged(messages[colour], PIECE, 0)
        other = swap(mine, Y_PAIRS)
        fresh.append(updated(owns[colour], mine, other))

    row_mine = row_keep + row_other
    row_far = swap(row_mine, HI_PAIRS)
    half = load_update(counts, row_base, row_mine, row_far)
    new_loadings = joined(half, swap(half, CORE_PAIRS))

    for step in (3, 2, 1):
        for colour in range(2):
            other = swap(fresh[colour], cube_pairs(colour, step))
            fresh[colour] = jnp.concatenate([fresh[colour], other], axis=0)
    last = [swap(fresh[colour], cube_pairs(colour, 0)) for colour in range(2)]
    new_profiles = stored(0, fresh[0], fresh[1])
    new_profiles = stored(8, last[0], last[1], new_profiles)
    return new_loadings, new_profiles


def solution(mesh):
    return jax.shard_map(
        local,
        mesh=mesh,
        in_specs=(P("curves", "tm"), P("curves", None), P("tm", None), P()),
        out_specs=(P("curves", None), P("tm", None)),
        check_vma=False,
    )
```

```python
import functools

import jax
import jax.numpy as jnp
from jax import lax
from jax.experimental import pallas as pl
from jax.experimental.pallas import tpu as pltpu
from jax.sharding import PartitionSpec as P


ROWS = 768
COMPS = 256
POINTS = 4096
COLOUR = POINTS // 2
TILE = 512
PIECE = COLOUR // 8
HALF = ROWS // 2
PAD = 8
F32 = jnp.float32
BF16 = jnp.bfloat16

ORDER = {(0, 0): (0, 1, 2, 3), (0, 1): (1, 0, 3, 2), (1, 0): (2, 3, 0, 1), (1, 1): (3, 2, 1, 0)}


def flip(bit, x, z):
    if bit == 0:
        return x ^ 1, z
    if bit == 1:
        return 3 - x, z
    if bit == 2:
        return x, z ^ 1
    return x, 3 - z


def pairs(move):
    out = []
    for x in range(4):
        for y in range(2):
            for z in range(4):
                for hi in range(2):
                    for core in range(2):
                        tx, ty, tz, thi, tcore = move(x, y, z, hi, core)
                        source = (x * 8 + y * 4 + z) * 4 + hi * 2 + core
                        target = (tx * 8 + ty * 4 + tz) * 4 + thi * 2 + tcore
                        out.append((source, target))
    return out


def cube_pairs(colour, step):
    def move(x, y, z, hi, core):
        tx, tz = flip(ORDER[core, colour][step], x, z)
        return tx, y, tz, hi, core

    return pairs(move)


Y_PAIRS = pairs(lambda x, y, z, hi, core: (x, 1 - y, z, hi, core))
HI_PAIRS = pairs(lambda x, y, z, hi, core: (x, y, z, 1 - hi, core))
CORE_PAIRS = pairs(lambda x, y, z, hi, core: (x, y, z, hi, 1 - core))


def swap(value, table):
    return lax.ppermute(value, ("curves", "tm"), table)


def my_label():
    index = lax.axis_index("curves")
    x, z = index // 8, index % 4
    return (x ^ (x >> 1)) | ((z ^ (z >> 1)) << 2)


def my_core():
    return lax.axis_index("tm") % 2


def my_piece(colour):
    label = my_label()
    views = []
    for core in range(2):
        order = ORDER[core, colour]
        views.append(sum(((label >> order[i]) & 1) << (2 - i) for i in range(3)))
    return jnp.where(my_core() == 0, views[0], views[1])


def split(value):
    high = value.astype(BF16)
    return high, (value - high.astype(F32)).astype(BF16)


def dot(a, b):
    return jnp.dot(a, b, preferred_element_type=F32)


def time_kernel(colour, counts, data, load, prof, send, keep, own, work, left, gram):
    step = pl.program_id(0)
    mine = my_piece(colour)

    @pl.when(step == 0)
    def _():
        live = counts[lax.axis_index("curves")]
        alive = lax.broadcasted_iota(jnp.int32, (ROWS, COMPS), 0) < live
        weights = jnp.where(alive, load[...], 0.0)
        high, low = split(weights)
        high_t, low_t = high.T, low.T
        left[:, :ROWS] = high_t
        left[:, ROWS : 2 * ROWS] = low_t
        left[:, 2 * ROWS :] = high_t
        both = dot(left[...], jnp.concatenate([high, high, low], axis=0))
        ghigh, glow = split(both)
        gram[:COMPS] = ghigh
        gram[COMPS : 2 * COMPS] = ghigh
        gram[2 * COMPS :] = glow
        norm = jnp.sum(weights * weights, axis=0, keepdims=True)
        norm = jnp.broadcast_to(norm, (PAD, COMPS))
        send[4 * PIECE :] = norm
        keep[4 * PIECE :] = norm

    for part in range(TILE // PIECE):
        high, low = split(data[:, part * PIECE : (part + 1) * PIECE])
        back = dot(left[...], jnp.concatenate([high, high, low], axis=0))
        phigh, plow = split(prof[part * PIECE : (part + 1) * PIECE])
        fitted = dot(jnp.concatenate([phigh, plow, phigh], axis=1), gram[...])
        position = (step * (TILE // PIECE) + part) ^ mine
        start = pl.multiple_of(position * PIECE, PIECE)
        work[pl.ds(start, PIECE)] = back.T - fitted

    for part in range(TILE // PIECE):

        @pl.when(step * (TILE // PIECE) + part == mine)
        def _():
            own[...] = prof[part * PIECE : (part + 1) * PIECE]

    @pl.when(step == pl.num_programs(0) - 1)
    def _():
        keep[: 4 * PIECE] = work[: 4 * PIECE]
        send[: 4 * PIECE] = work[4 * PIECE :]


def time_part(colour, counts, data, load, prof):
    steps = COLOUR // TILE
    base = colour * steps
    message = jax.ShapeDtypeStruct((4 * PIECE + PAD, COMPS), F32)
    whole = pl.BlockSpec((4 * PIECE + PAD, COMPS), lambda i, c: (0, 0))
    return pl.pallas_call(
        functools.partial(time_kernel, colour),
        out_shape=(message, message, jax.ShapeDtypeStruct((PIECE, COMPS), F32)),
        grid_spec=pltpu.PrefetchScalarGridSpec(
            num_scalar_prefetch=1,
            grid=(steps,),
            in_specs=[
                pl.BlockSpec((ROWS, TILE), lambda i, c: (0, base + i)),
                pl.BlockSpec((ROWS, COMPS), lambda i, c: (0, 0)),
                pl.BlockSpec((TILE, COMPS), lambda i, c: (base + i, 0)),
            ],
            out_specs=(whole, whole, pl.BlockSpec((PIECE, COMPS), lambda i, c: (0, 0))),
            scratch_shapes=[
                pltpu.VMEM((COLOUR, COMPS), F32),
                pltpu.VMEM((COMPS, 3 * ROWS), BF16),
                pltpu.VMEM((3 * COMPS, COMPS), BF16),
            ],
        ),
        compiler_params=pltpu.CompilerParams(vmem_limit_bytes=54 << 20),
        cost_estimate=pl.CostEstimate(
            flops=6 * COLOUR * COMPS * (ROWS + COMPS), bytes_accessed=4 * COLOUR * (ROWS + 2 * COMPS), transcendentals=0
        ),
    )(counts, data, load, prof)


def row_sums(data, prof, total, gram, norm):
    high, low = split(data[...])
    points = prof[...]
    phigh, plow = split(points)
    total[...] += dot(
        jnp.concatenate([high, low, high], axis=1), jnp.concatenate([phigh, phigh, plow], axis=0)
    )
    gram[...] += dot(phigh.T, jnp.concatenate([phigh, plow], axis=1))
    norm[...] += jnp.broadcast_to(jnp.sum(points * points, axis=0, keepdims=True), norm.shape)


def early_kernel(data, prof, total, gram, norm):
    @pl.when(pl.program_id(0) == 0)
    def _():
        total[...] = jnp.zeros_like(total)
        gram[...] = jnp.zeros_like(gram)
        norm[...] = jnp.zeros_like(norm)

    row_sums(data, prof, total, gram, norm)


def late_kernel(data, load, prof, total_in, gram_in, norm_in, send, keep, base, total, gram, norm):
    @pl.when(pl.program_id(0) == 0)
    def _():
        total[...] = total_in[...]
        gram[...] = gram_in[...]
        norm[...] = norm_in[...]

    row_sums(data, prof, total, gram, norm)

    @pl.when(pl.program_id(0) == pl.num_programs(0) - 1)
    def _():
        mixed = gram[:, COMPS:]
        ghigh, glow = split(gram[:, :COMPS] + mixed + mixed.T)
        high, low = split(load[...])
        total[...] -= dot(jnp.concatenate([high, low, high], axis=1), jnp.concatenate([ghigh, ghigh, glow], axis=0))
        mine = pl.multiple_of(my_core() * HALF, HALF)
        other = pl.multiple_of(HALF - my_core() * HALF, HALF)
        send[:HALF] = total[pl.ds(other, HALF)]
        keep[:HALF] = total[pl.ds(mine, HALF)]
        send[HALF:] = norm[...]
        keep[HALF:] = norm[...]
        base[...] = load[pl.ds(mine, HALF)]


SUMS = ((ROWS, COMPS), (COMPS, 2 * COMPS), (PAD, COMPS))


def row_part(stage, data, load, prof, sums=()):
    steps = POINTS // 2 // TILE
    base = stage * steps
    fixed = lambda shape: pl.BlockSpec(shape, lambda i: (0, 0))
    specs = [pl.BlockSpec((ROWS, TILE), lambda i: (0, base + i)), pl.BlockSpec((TILE, COMPS), lambda i: (base + i, 0))]
    if stage == 0:
        kernel, shapes, scratch, args = early_kernel, SUMS, [], (data, prof)
    else:
        kernel, shapes = late_kernel, ((HALF + PAD, COMPS), (HALF + PAD, COMPS), (HALF, COMPS))
        scratch = [pltpu.VMEM(shape, F32) for shape in SUMS]
        args = (data, load, prof, *sums)
        specs = [specs[0], fixed((ROWS, COMPS)), specs[1], *(fixed(shape) for shape in SUMS)]
    return pl.pallas_call(
        kernel,
        out_shape=tuple(jax.ShapeDtypeStruct(shape, F32) for shape in shapes),
        grid=(steps,),
        in_specs=specs,
        out_specs=tuple(fixed(shape) for shape in shapes),
        scratch_shapes=scratch,
        compiler_params=pltpu.CompilerParams(vmem_limit_bytes=54 << 20),
        cost_estimate=pl.CostEstimate(
            flops=3 * POINTS * COMPS * (ROWS + COMPS), bytes_accessed=2 * POINTS * (ROWS + COMPS), transcendentals=0
        ),
    )(*args)


def merged(messages, rows, index):
    add = lambda parts: functools.reduce(lambda a, b: a + b, parts)
    piece = add([m[index * rows : (index + 1) * rows] for m in messages])
    return jnp.concatenate([piece, add([m[-PAD:] for m in messages])], axis=0)


def updated(base, mine, other):
    rows = base.shape[0]
    grad = mine[:rows] + other[:rows]
    norm = mine[rows : rows + 1] + other[rows : rows + 1]
    return jnp.maximum(base + grad / norm, 0.0)


def load_kernel(counts, base, mine, other, out):
    rows = out.shape[0]
    grad = mine[:rows] + other[:rows]
    norm = mine[rows : rows + 1] + other[rows : rows + 1]
    fresh = jnp.maximum(base[...] + grad / norm, 0.0)
    slot = lax.broadcasted_iota(jnp.int32, fresh.shape, 0) + my_core() * HALF
    out[...] = jnp.where(slot < counts[lax.axis_index("curves")], fresh, 0.0)


def load_update(counts, base, mine, other):
    vmem = pl.BlockSpec(memory_space=pltpu.VMEM)
    return pl.pallas_call(
        load_kernel,
        out_shape=jax.ShapeDtypeStruct(base.shape, F32),
        in_specs=[pl.BlockSpec(memory_space=pltpu.SMEM), vmem, vmem, vmem],
        cost_estimate=pl.CostEstimate(flops=4 * base.size, bytes_accessed=16 * base.size, transcendentals=0),
        compiler_params=pltpu.CompilerParams(vmem_limit_bytes=8 << 20),
        name="load_update",
    )(counts, base, mine, other)


def join_kernel(mine, other, out, sems):
    core = my_core()
    first = pltpu.make_async_copy(mine, out.at[pl.ds(pl.multiple_of(core * HALF, HALF), HALF)], sems.at[0])
    second = pltpu.make_async_copy(other, out.at[pl.ds(pl.multiple_of(HALF - core * HALF, HALF), HALF)], sems.at[1])
    first.start()
    second.start()
    first.wait()
    second.wait()


def joined(mine, other):
    vmem = pl.BlockSpec(memory_space=pltpu.VMEM)
    return pl.pallas_call(
        join_kernel,
        out_shape=jax.ShapeDtypeStruct((ROWS, COMPS), F32),
        in_specs=[vmem, vmem],
        out_specs=pl.BlockSpec(memory_space=pl.ANY),
        scratch_shapes=[pltpu.SemaphoreType.DMA((2,))],
        compiler_params=pltpu.CompilerParams(vmem_limit_bytes=8 << 20),
        name="joined",
    )(mine, other)


def store_kernel(first, *refs):
    left, right = refs[0], refs[1]
    out, sems = refs[-2], refs[-1]
    copies = []
    for colour, source in enumerate((left, right)):
        for i in range(4):
            piece = (first + i) ^ my_piece(colour)
            start = pl.multiple_of(colour * COLOUR + piece * PIECE, PIECE)
            copies.append(
                pltpu.make_async_copy(
                    source.at[pl.ds(i * PIECE, PIECE)], out.at[pl.ds(start, PIECE)], sems.at[colour * 4 + i]
                )
            )
    for copy in copies:
        copy.start()
    for copy in copies:
        copy.wait()


def stored(first, left, right, held=None):
    vmem = pl.BlockSpec(memory_space=pltpu.VMEM)
    args, specs, alias = [left, right], [vmem, vmem], {}
    if held is not None:
        args.append(held)
        specs.append(pl.BlockSpec(memory_space=pl.ANY))
        alias = {2: 0}
    return pl.pallas_call(
        functools.partial(store_kernel, first),
        out_shape=jax.ShapeDtypeStruct((POINTS, COMPS), F32),
        in_specs=specs,
        out_specs=pl.BlockSpec(memory_space=pl.ANY),
        scratch_shapes=[pltpu.SemaphoreType.DMA((8,))],
        input_output_aliases=alias,
        compiler_params=pltpu.CompilerParams(vmem_limit_bytes=8 << 20),
        cost_estimate=pl.CostEstimate(flops=0, bytes_accessed=16 * left.size, transcendentals=0),
        name="stored",
    )(*args)


def local(curves_data, loadings, profiles, counts):
    messages, owns = [], []
    for colour in range(2):
        send, keep, own = time_part(colour, counts, curves_data, loadings, profiles)
        messages.append([keep, swap(send, cube_pairs(colour, 0))])
        owns.append(own)
    sums = row_part(0, curves_data, loadings, profiles)
    row_send, row_keep, row_base = row_part(1, curves_data, loadings, profiles, sums)
    row_other = swap(row_send, CORE_PAIRS)

    rows = 2 * PIECE
    for step in range(1, 3):
        for colour in range(2):
            send = merged(messages[colour], rows, 1)
            messages[colour].append(swap(send, cube_pairs(colour, step)))
        rows //= 2
    mine = [merged(messages[colour], PIECE, 0) for colour in range(2)]
    far = [swap(mine[colour], cube_pairs(colour, 3)) for colour in range(2)]
    mine = [mine[colour] + far[colour] for colour in range(2)]
    far = [swap(mine[colour], Y_PAIRS) for colour in range(2)]
    fresh = [updated(owns[colour], mine[colour], far[colour]) for colour in range(2)]

    row_mine = row_keep + row_other
    row_far = swap(row_mine, HI_PAIRS)
    half = load_update(counts, row_base, row_mine, row_far)
    new_loadings = joined(half, swap(half, CORE_PAIRS))

    for step in (2, 1):
        for colour in range(2):
            other = swap(fresh[colour], cube_pairs(colour, step))
            fresh[colour] = jnp.concatenate([fresh[colour], other], axis=0)
    last = [swap(fresh[colour], cube_pairs(colour, 0)) for colour in range(2)]
    new_profiles = stored(0, fresh[0], fresh[1])
    new_profiles = stored(4, last[0], last[1], new_profiles)
    return new_loadings, new_profiles


def solution(mesh):
    return jax.shard_map(
        local,
        mesh=mesh,
        in_specs=(P("curves", "tm"), P("curves", None), P("tm", None), P()),
        out_specs=(P("curves", None), P("tm", None)),
        check_vma=False,
    )
```

```python
import functools

import jax
import jax.numpy as jnp
from jax import lax
from jax.experimental import pallas as pl
from jax.experimental.pallas import tpu as pltpu
from jax.sharding import PartitionSpec as P


ROWS = 768
COMPS = 256
POINTS = 4096
COLOUR = POINTS // 2
PIECE = COLOUR // 8
HALF = ROWS // 2
PAD = 8
GRANT = 20 << 20
F32 = jnp.float32
BF16 = jnp.bfloat16

ORDER = {(0, 0): (0, 1, 2, 3), (0, 1): (1, 0, 2, 3), (1, 0): (2, 3, 0, 1), (1, 1): (3, 2, 0, 1)}


def flip(bit, x, z):
    if bit == 0:
        return x ^ 1, z
    if bit == 1:
        return 3 - x, z
    if bit == 2:
        return x, z ^ 1
    return x, 3 - z


def pairs(move):
    out = []
    for x in range(4):
        for y in range(2):
            for z in range(4):
                for hi in range(2):
                    for core in range(2):
                        tx, ty, tz, thi, tcore = move(x, y, z, hi, core)
                        source = (x * 8 + y * 4 + z) * 4 + hi * 2 + core
                        target = (tx * 8 + ty * 4 + tz) * 4 + thi * 2 + tcore
                        out.append((source, target))
    return out


def cube_pairs(colour, step):
    def move(x, y, z, hi, core):
        tx, tz = flip(ORDER[core, colour][step], x, z)
        return tx, y, tz, hi, core

    return pairs(move)


Y_PAIRS = pairs(lambda x, y, z, hi, core: (x, 1 - y, z, hi, core))
HI_PAIRS = pairs(lambda x, y, z, hi, core: (x, y, z, 1 - hi, core))
CORE_PAIRS = pairs(lambda x, y, z, hi, core: (x, y, z, hi, 1 - core))


def swap(value, table):
    return lax.ppermute(value, ("curves", "tm"), table)


def my_label():
    index = lax.axis_index("curves")
    x, z = index // 8, index % 4
    return (x ^ (x >> 1)) | ((z ^ (z >> 1)) << 2)


def my_core():
    return lax.axis_index("tm") % 2


def my_piece(colour):
    label = my_label()
    views = []
    for core in range(2):
        order = ORDER[core, colour]
        views.append(sum(((label >> order[i]) & 1) << (2 - i) for i in range(3)))
    return jnp.where(my_core() == 0, views[0], views[1])


def split(value):
    high = value.astype(BF16)
    return high, (value - high.astype(F32)).astype(BF16)


def dot(a, b):
    return jnp.dot(a, b, preferred_element_type=F32)


def prepare(live, load, left, gram, norm):
    alive = lax.broadcasted_iota(jnp.int32, (ROWS, COMPS), 0) < live
    weights = jnp.where(alive, load[...], 0.0)
    high, low = split(weights)
    high_t, low_t = high.T, low.T
    left[:, :ROWS] = high_t
    left[:, ROWS : 2 * ROWS] = low_t
    left[:, 2 * ROWS :] = high_t
    ghigh, glow = split(dot(left[...], jnp.concatenate([high, high, low], axis=0)))
    gram[:COMPS] = ghigh
    gram[COMPS : 2 * COMPS] = ghigh
    gram[2 * COMPS :] = glow
    norm[...] = jnp.broadcast_to(jnp.sum(weights * weights, axis=0, keepdims=True), (PAD, COMPS))


def pair_start(colour, pair):
    return (pair ^ (my_piece(colour) >> 1)) * 2


def time_sums(colour, piece, data, prof, left, gram, out):
    high, low = split(data)
    back = dot(left[...], jnp.concatenate([high, high, low], axis=0))
    phigh, plow = split(prof)
    fitted = dot(jnp.concatenate([phigh, plow, phigh], axis=1), gram[...])
    start = pl.multiple_of(((piece ^ my_piece(colour)) & 1) * PIECE, PIECE)
    out[pl.ds(start, PIECE)] = back.T - fitted


def first_kernel(counts, data, load, prof, send, left, gram, norm, live, block, weights, points, sems):
    pair = pair_start(0, 3)
    start = pl.multiple_of(pair * PIECE, 2 * PIECE)
    copies = [
        pltpu.make_async_copy(counts, live, sems.at[0]),
        pltpu.make_async_copy(load, weights, sems.at[1]),
        pltpu.make_async_copy(data.at[:, pl.ds(start, 2 * PIECE)], block, sems.at[2]),
        pltpu.make_async_copy(prof.at[pl.ds(start, 2 * PIECE)], points, sems.at[3]),
    ]
    for copy in copies:
        copy.start()
    copies[0].wait()
    copies[1].wait()
    prepare(live[lax.axis_index("curves")], weights, left, gram, norm)
    copies[2].wait()
    copies[3].wait()
    for i in range(2):
        part = slice(i * PIECE, (i + 1) * PIECE)
        time_sums(0, pair + i, block[:, part], points[part], left, gram, send)
    send[2 * PIECE :] = norm[...]


def pair_sums(colour, pair, data, prof, left, gram, out):
    for i in range(2):
        piece = pair_start(colour, pair) + i
        points = pl.ds(pl.multiple_of(colour * COLOUR + piece * PIECE, PIECE), PIECE)
        time_sums(colour, piece, data[:, points], prof[points], left, gram, out)


def send_kernel(colour, pair, data, prof, left, gram, norm, send):
    pair_sums(colour, pair, data, prof, left, gram, send)
    if pair == 3:
        send[2 * PIECE :] = norm[...]


def keep_kernel(pair, data, prof, left, gram, keep0, keep1, *owns):
    for colour, keep in enumerate((keep0, keep1)):
        pair_sums(colour, pair, data, prof, left, gram, keep)
        if owns:
            start = pl.multiple_of(colour * COLOUR + my_piece(colour) * PIECE, PIECE)
            owns[colour][...] = prof[pl.ds(start, PIECE)]


VMEM = pl.BlockSpec(memory_space=pltpu.VMEM)
PAIR = jax.ShapeDtypeStruct((2 * PIECE, COMPS), F32)
MESSAGE = jax.ShapeDtypeStruct((2 * PIECE + PAD, COMPS), F32)
SHARED = (
    jax.ShapeDtypeStruct((COMPS, 3 * ROWS), BF16),
    jax.ShapeDtypeStruct((3 * COMPS, COMPS), BF16),
    jax.ShapeDtypeStruct((PAD, COMPS), F32),
)


def time_part(kind, colour, pair, data, prof, shared=(), counts=None, load=None):
    pieces, scratch = (4 if kind == "keep" else 2), []
    if kind == "first":
        kernel, shapes = first_kernel, (MESSAGE, *SHARED)
        args = tuple(pltpu.with_memory_space_constraint(arg, pltpu.HBM) for arg in (counts, data, load, prof))
        specs = [pl.BlockSpec(memory_space=pltpu.HBM)] * 4
        scratch = [
            pltpu.SMEM(counts.shape, jnp.int32),
            pltpu.VMEM((ROWS, 2 * PIECE), F32),
            pltpu.VMEM((ROWS, COMPS), F32),
            pltpu.VMEM((2 * PIECE, COMPS), F32),
            pltpu.SemaphoreType.DMA((4,)),
        ]
    elif kind == "send":
        kernel, args = functools.partial(send_kernel, colour, pair), (data, prof, *shared)
        shapes = (MESSAGE if pair == 3 else PAIR,)
        specs = [VMEM] * 5
    else:
        own = jax.ShapeDtypeStruct((PIECE, COMPS), F32)
        kernel, args = functools.partial(keep_kernel, pair), (data, prof, *shared[:2])
        shapes = (PAIR, PAIR) if pair else (PAIR, PAIR, own, own)
        specs = [VMEM] * 4
    return pl.pallas_call(
        kernel,
        out_shape=shapes,
        in_specs=specs,
        out_specs=tuple(VMEM for _ in shapes),
        scratch_shapes=scratch,
        compiler_params=pltpu.CompilerParams(vmem_limit_bytes=GRANT),
        cost_estimate=pl.CostEstimate(
            flops=6 * pieces * PIECE * COMPS * (ROWS + COMPS),
            bytes_accessed=4 * pieces * PIECE * (ROWS + 2 * COMPS),
            transcendentals=0,
        ),
    )(*args)


def row_sums(stage, data, prof):
    size = POINTS // STAGES
    points = slice(stage * size, (stage + 1) * size)
    high, low = split(data[:, points])
    part = prof[points]
    phigh, plow = split(part)
    total = dot(jnp.concatenate([high, low, high], axis=1), jnp.concatenate([phigh, phigh, plow], axis=0))
    gram = dot(phigh.T, jnp.concatenate([phigh, plow], axis=1))
    norm = jnp.broadcast_to(jnp.sum(part * part, axis=0, keepdims=True), (PAD, COMPS))
    return total, gram, norm


def early_kernel(data, prof, *sums):
    for out, value in zip(sums, row_sums(0, data, prof)):
        out[...] = value


def middle_kernel(stage, data, prof, *refs):
    for old, out, value in zip(refs[:3], refs[3:], row_sums(stage, data, prof)):
        out[...] = old[...] + value


def late_kernel(data, load, prof, total_in, gram_in, norm_in, send, keep, base, total):
    more, gram, norm = row_sums(STAGES - 1, data, prof)
    gram += gram_in[...]
    norm += norm_in[...]
    mixed = gram[:, COMPS:]
    ghigh, glow = split(gram[:, :COMPS] + mixed + mixed.T)
    high, low = split(load[...])
    fitted = dot(jnp.concatenate([high, low, high], axis=1), jnp.concatenate([ghigh, ghigh, glow], axis=0))
    total[...] = total_in[...] + more - fitted
    mine = pl.multiple_of(my_core() * HALF, HALF)
    other = pl.multiple_of(HALF - my_core() * HALF, HALF)
    send[:HALF] = total[pl.ds(other, HALF)]
    keep[:HALF] = total[pl.ds(mine, HALF)]
    send[HALF:] = norm
    keep[HALF:] = norm
    base[...] = load[pl.ds(mine, HALF)]


SUMS = tuple(jax.ShapeDtypeStruct(shape, F32) for shape in ((ROWS, COMPS), (COMPS, 2 * COMPS), (PAD, COMPS)))
STAGES = 8


def row_part(stage, data, load, prof, sums=()):
    alias, scratch = {}, []
    if stage == 0:
        kernel, shapes, args = early_kernel, SUMS, (data, prof)
    elif stage < STAGES - 1:
        kernel, shapes, args = functools.partial(middle_kernel, stage), SUMS, (data, prof, *sums)
        alias = {2: 0, 3: 1, 4: 2}
    else:
        message = jax.ShapeDtypeStruct((HALF + PAD, COMPS), F32)
        kernel, shapes = late_kernel, (message, message, jax.ShapeDtypeStruct((HALF, COMPS), F32))
        args, scratch = (data, load, prof, *sums), [pltpu.VMEM((ROWS, COMPS), F32)]
    return pl.pallas_call(
        kernel,
        out_shape=shapes,
        in_specs=[VMEM] * len(args),
        out_specs=tuple(VMEM for _ in shapes),
        scratch_shapes=scratch,
        input_output_aliases=alias,
        compiler_params=pltpu.CompilerParams(vmem_limit_bytes=GRANT),
        cost_estimate=pl.CostEstimate(
            flops=6 * POINTS // STAGES * COMPS * (ROWS + COMPS),
            bytes_accessed=4 * POINTS // STAGES * (ROWS + COMPS),
            transcendentals=0,
        ),
    )(*args)


def joined_up(pieces, norms):
    add = lambda parts: functools.reduce(lambda a, b: a + b, parts)
    return jnp.concatenate([add(pieces), add(norms)], axis=0)


def updated(base, mine, other):
    rows = base.shape[0]
    grad = mine[:rows] + other[:rows]
    norm = mine[rows : rows + 1] + other[rows : rows + 1]
    return jnp.maximum(base + grad / norm, 0.0)


def load_kernel(counts, base, mine, other, out):
    rows = out.shape[0]
    grad = mine[:rows] + other[:rows]
    norm = mine[rows : rows + 1] + other[rows : rows + 1]
    fresh = jnp.maximum(base[...] + grad / norm, 0.0)
    slot = lax.broadcasted_iota(jnp.int32, fresh.shape, 0) + my_core() * HALF
    out[...] = jnp.where(slot < counts[lax.axis_index("curves")], fresh, 0.0)


def load_update(counts, base, mine, other):
    return pl.pallas_call(
        load_kernel,
        out_shape=jax.ShapeDtypeStruct(base.shape, F32),
        in_specs=[pl.BlockSpec(memory_space=pltpu.SMEM), VMEM, VMEM, VMEM],
        cost_estimate=pl.CostEstimate(flops=4 * base.size, bytes_accessed=16 * base.size, transcendentals=0),
        compiler_params=pltpu.CompilerParams(vmem_limit_bytes=8 << 20),
        name="load_update",
    )(counts, base, mine, other)


def join_kernel(mine, other, out, sems):
    core = my_core()
    first = pltpu.make_async_copy(mine, out.at[pl.ds(pl.multiple_of(core * HALF, HALF), HALF)], sems.at[0])
    second = pltpu.make_async_copy(other, out.at[pl.ds(pl.multiple_of(HALF - core * HALF, HALF), HALF)], sems.at[1])
    first.start()
    second.start()
    first.wait()
    second.wait()


def joined(mine, other):
    return pl.pallas_call(
        join_kernel,
        out_shape=jax.ShapeDtypeStruct((ROWS, COMPS), F32),
        in_specs=[VMEM, VMEM],
        out_specs=pl.BlockSpec(memory_space=pl.ANY),
        scratch_shapes=[pltpu.SemaphoreType.DMA((2,))],
        compiler_params=pltpu.CompilerParams(vmem_limit_bytes=8 << 20),
        name="joined",
    )(mine, other)


def store_kernel(places, *refs):
    out, sems = refs[-2], refs[-1]
    copies = []
    for source, (colour, pair) in zip(refs, places):
        for i in range(2):
            piece = (2 * pair + i) ^ my_piece(colour)
            start = pl.multiple_of(colour * COLOUR + piece * PIECE, PIECE)
            copies.append(
                pltpu.make_async_copy(
                    source.at[pl.ds(i * PIECE, PIECE)], out.at[pl.ds(start, PIECE)], sems.at[len(copies)]
                )
            )
    for copy in copies:
        copy.start()
    for copy in copies:
        copy.wait()


def stored(places, sources, held=None):
    args, specs, alias = list(sources), [VMEM] * len(sources), {}
    if held is not None:
        alias = {len(args): 0}
        args.append(held)
        specs.append(pl.BlockSpec(memory_space=pl.ANY))
    return pl.pallas_call(
        functools.partial(store_kernel, places),
        out_shape=jax.ShapeDtypeStruct((POINTS, COMPS), F32),
        in_specs=specs,
        out_specs=pl.BlockSpec(memory_space=pl.ANY),
        scratch_shapes=[pltpu.SemaphoreType.DMA((2 * len(places),))],
        input_output_aliases=alias,
        compiler_params=pltpu.CompilerParams(vmem_limit_bytes=8 << 20),
        cost_estimate=pl.CostEstimate(flops=0, bytes_accessed=16 * PIECE * COMPS * len(places), transcendentals=0),
        name="stored",
    )(*args)


def local(curves_data, loadings, profiles, counts):
    both = range(2)
    hop = lambda c, value, step: swap(value, cube_pairs(c, step))
    send, *shared = time_part("first", 0, 3, curves_data, profiles, (), counts, loadings)
    norm = shared[2]
    early = [hop(0, send, 0)]
    (send,) = time_part("send", 1, 3, curves_data, profiles, shared)
    early.append(hop(1, send, 0))
    (send,) = time_part("send", 0, 2, curves_data, profiles, shared)
    late = [hop(0, send, 0)]
    (send,) = time_part("send", 1, 2, curves_data, profiles, shared)
    late.append(hop(1, send, 0))
    high = time_part("keep", 0, 1, curves_data, profiles, shared)
    *low, own0, own1 = time_part("keep", 0, 0, curves_data, profiles, shared)
    owns = [own0, own1]
    sums = ()
    for stage in range(STAGES):
        sums = row_part(stage, curves_data, loadings, profiles, sums)
    row_send, row_keep, row_base = sums[:3]
    row_other = swap(row_send, CORE_PAIRS)

    norms = [[norm, early[c][-PAD:]] for c in both]
    mid = [hop(c, joined_up([high[c], early[c][:-PAD]], norms[c]), 1) for c in both]
    norms = [norms[c] + [mid[c][-PAD:]] for c in both]
    one, zero = slice(PIECE, 2 * PIECE), slice(0, PIECE)
    last = [hop(c, joined_up([low[c][one], late[c][one], mid[c][one]], norms[c]), 2) for c in both]
    norms = [norms[c] + [last[c][-PAD:]] for c in both]
    mine = [joined_up([m[c][zero] for m in (low, late, mid, last)], norms[c]) for c in both]
    far = [hop(c, mine[c], 3) for c in both]
    mine = [mine[c] + far[c] for c in both]
    far = [swap(mine[c], Y_PAIRS) for c in both]
    fresh = [updated(owns[c], mine[c], far[c]) for c in both]

    row_mine = row_keep + row_other
    row_far = swap(row_mine, HI_PAIRS)
    half = load_update(counts, row_base, row_mine, row_far)
    new_loadings = joined(half, swap(half, CORE_PAIRS))

    near = [jnp.concatenate([fresh[c], hop(c, fresh[c], 2)], axis=0) for c in both]
    next_pair = [hop(c, near[c], 1) for c in both]
    third = [hop(c, near[c], 0) for c in both]
    fourth = [hop(c, next_pair[c], 0) for c in both]
    new_profiles = stored(((0, 0), (1, 0), (0, 1), (1, 1)), near + next_pair)
    new_profiles = stored(((0, 2), (1, 2)), third, new_profiles)
    new_profiles = stored(((0, 3), (1, 3)), fourth, new_profiles)
    return new_loadings, new_profiles


def solution(mesh):
    return jax.shard_map(
        local,
        mesh=mesh,
        in_specs=(P("curves", "tm"), P("curves", None), P("tm", None), P()),
        out_specs=(P("curves", None), P("tm", None)),
        check_vma=False,
    )
```

```python
import functools

import jax
import jax.numpy as jnp
from jax import lax
from jax.experimental import pallas as pl
from jax.experimental.pallas import tpu as pltpu
from jax.sharding import PartitionSpec as P


ROWS = 768
COMPS = 256
POINTS = 4096
COLOUR = POINTS // 2
PIECE = COLOUR // 8
PAD = 8
GRANT = 20 << 20
F32 = jnp.float32
BF16 = jnp.bfloat16

ORDER = {(0, 0): (0, 1, 2, 3), (0, 1): (1, 0, 2, 3), (1, 0): (2, 3, 0, 1), (1, 1): (3, 2, 0, 1)}


def flip(bit, x, z):
    if bit == 0:
        return x ^ 1, z
    if bit == 1:
        return 3 - x, z
    if bit == 2:
        return x, z ^ 1
    return x, 3 - z


def pairs(move):
    out = []
    for x in range(4):
        for y in range(2):
            for z in range(4):
                for hi in range(2):
                    for core in range(2):
                        tx, ty, tz, thi, tcore = move(x, y, z, hi, core)
                        source = (x * 8 + y * 4 + z) * 4 + hi * 2 + core
                        target = (tx * 8 + ty * 4 + tz) * 4 + thi * 2 + tcore
                        out.append((source, target))
    return out


def cube_pairs(colour, step):
    def move(x, y, z, hi, core):
        tx, tz = flip(ORDER[core, colour][step], x, z)
        return tx, y, tz, hi, core

    return pairs(move)


Y_PAIRS = pairs(lambda x, y, z, hi, core: (x, 1 - y, z, hi, core))
HI_PAIRS = pairs(lambda x, y, z, hi, core: (x, y, z, 1 - hi, core))
CORE_PAIRS = pairs(lambda x, y, z, hi, core: (x, y, z, hi, 1 - core))


def swap(value, table):
    return lax.ppermute(value, ("curves", "tm"), table)


def my_label():
    index = lax.axis_index("curves")
    x, z = index // 8, index % 4
    return (x ^ (x >> 1)) | ((z ^ (z >> 1)) << 2)


def my_core():
    return lax.axis_index("tm") % 2


def my_piece(colour):
    label = my_label()
    views = []
    for core in range(2):
        order = ORDER[core, colour]
        views.append(sum(((label >> order[i]) & 1) << (2 - i) for i in range(3)))
    return jnp.where(my_core() == 0, views[0], views[1])


def split(value):
    high = value.astype(BF16)
    return high, (value - high.astype(F32)).astype(BF16)


def dot(a, b):
    return jnp.dot(a, b, preferred_element_type=F32)


def prepare(live, load, left, gram, norms):
    alive = lax.broadcasted_iota(jnp.int32, (ROWS, COMPS), 0) < live
    weights = jnp.where(alive, load[...], 0.0)
    high, low = split(weights)
    high_t, low_t = high.T, low.T
    left[:, :ROWS] = high_t
    left[:, ROWS : 2 * ROWS] = low_t
    left[:, 2 * ROWS :] = high_t
    ghigh, glow = split(dot(left[...], jnp.concatenate([high, high, low], axis=0)))
    gram[:COMPS] = ghigh
    gram[COMPS : 2 * COMPS] = ghigh
    gram[2 * COMPS :] = glow
    total = jnp.broadcast_to(jnp.sum(weights * weights, axis=0, keepdims=True), (PAD, COMPS))
    for norm in norms:
        norm[...] = total


def pair_start(colour, pair):
    return (pair ^ (my_piece(colour) >> 1)) * 2


def time_sums(colour, piece, data, prof, left, gram, out):
    high, low = split(data)
    back = dot(left[...], jnp.concatenate([high, high, low], axis=0))
    phigh, plow = split(prof)
    fitted = dot(jnp.concatenate([phigh, plow, phigh], axis=1), gram[...])
    start = pl.multiple_of(((piece ^ my_piece(colour)) & 1) * PIECE, PIECE)
    out[pl.ds(start, PIECE)] = back.T - fitted


def first_kernel(
    counts, data, load, prof, send, left, gram, norm0, norm1, block1, points1, live, block0, points0, weights, sems
):
    copies = [
        pltpu.make_async_copy(counts, live, sems.at[0]),
        pltpu.make_async_copy(load, weights, sems.at[1]),
    ]
    for colour, (block, points) in enumerate(((block0, points0), (block1, points1))):
        start = pl.multiple_of(colour * COLOUR + pair_start(colour, 3) * PIECE, 2 * PIECE)
        copies.append(pltpu.make_async_copy(data.at[:, pl.ds(start, 2 * PIECE)], block, sems.at[2 + 2 * colour]))
        copies.append(pltpu.make_async_copy(prof.at[pl.ds(start, 2 * PIECE)], points, sems.at[3 + 2 * colour]))
    for copy in copies:
        copy.start()
    copies[0].wait()
    copies[1].wait()
    prepare(live[lax.axis_index("curves")], weights, left, gram, (norm0, norm1))
    copies[2].wait()
    copies[3].wait()
    block_sums(0, block0, points0, left, gram, norm0, send)
    copies[4].wait()
    copies[5].wait()


def block_sums(colour, block, points, left, gram, norm, send):
    for i in range(2):
        part = slice(i * PIECE, (i + 1) * PIECE)
        time_sums(colour, pair_start(colour, 3) + i, block[:, part], points[part], left, gram, send)
    send[2 * PIECE :] = norm[...]


def second_kernel(block, points, left, gram, norm, send):
    block_sums(1, block, points, left, gram, norm, send)


def pair_sums(colour, pair, data, prof, left, gram, out):
    for i in range(2):
        piece = pair_start(colour, pair) + i
        points = pl.ds(pl.multiple_of(colour * COLOUR + piece * PIECE, PIECE), PIECE)
        time_sums(colour, piece, data[:, points], prof[points], left, gram, out)


def send_kernel(colour, pair, data, prof, left, gram, send):
    pair_sums(colour, pair, data, prof, left, gram, send)


def keep_kernel(pair, data, prof, left, gram, keep0, keep1, *owns):
    for colour, keep in enumerate((keep0, keep1)):
        pair_sums(colour, pair, data, prof, left, gram, keep)
        if owns:
            start = pl.multiple_of(colour * COLOUR + my_piece(colour) * PIECE, PIECE)
            owns[colour][...] = prof[pl.ds(start, PIECE)]


VMEM = pl.BlockSpec(memory_space=pltpu.VMEM)
PAIR = jax.ShapeDtypeStruct((2 * PIECE, COMPS), F32)
MESSAGE = jax.ShapeDtypeStruct((2 * PIECE + PAD, COMPS), F32)
SHARED = (
    jax.ShapeDtypeStruct((COMPS, 3 * ROWS), BF16),
    jax.ShapeDtypeStruct((3 * COMPS, COMPS), BF16),
    jax.ShapeDtypeStruct((PAD, COMPS), F32),
    jax.ShapeDtypeStruct((PAD, COMPS), F32),
    jax.ShapeDtypeStruct((ROWS, 2 * PIECE), F32),
    PAIR,
)


def time_part(kind, colour, pair, data, prof, shared=(), counts=None, load=None):
    pieces, scratch = (4 if kind == "keep" else 2), []
    if kind == "first":
        kernel, shapes = first_kernel, (MESSAGE, *SHARED)
        args = tuple(pltpu.with_memory_space_constraint(arg, pltpu.HBM) for arg in (counts, data, load, prof))
        specs = [pl.BlockSpec(memory_space=pltpu.HBM)] * 4
        scratch = [
            pltpu.SMEM(counts.shape, jnp.int32),
            pltpu.VMEM((ROWS, 2 * PIECE), F32),
            pltpu.VMEM((2 * PIECE, COMPS), F32),
            pltpu.VMEM((ROWS, COMPS), F32),
            pltpu.SemaphoreType.DMA((6,)),
        ]
    elif kind == "second":
        left, gram, _, norm, block, points = shared
        kernel, shapes, args = second_kernel, (MESSAGE,), (block, points, left, gram, norm)
        specs = [VMEM] * 5
    elif kind == "send":
        kernel, args = functools.partial(send_kernel, colour, pair), (data, prof, *shared[:2])
        shapes, specs = (PAIR,), [VMEM] * 4
    else:
        own = jax.ShapeDtypeStruct((PIECE, COMPS), F32)
        kernel, args = functools.partial(keep_kernel, pair), (data, prof, *shared[:2])
        shapes = (PAIR, PAIR) if pair else (PAIR, PAIR, own, own)
        specs = [VMEM] * 4
    return pl.pallas_call(
        kernel,
        out_shape=shapes,
        in_specs=specs,
        out_specs=tuple(VMEM for _ in shapes),
        scratch_shapes=scratch,
        compiler_params=pltpu.CompilerParams(vmem_limit_bytes=GRANT),
        cost_estimate=pl.CostEstimate(
            flops=6 * pieces * PIECE * COMPS * (ROWS + COMPS),
            bytes_accessed=4 * pieces * PIECE * (ROWS + 2 * COMPS),
            transcendentals=0,
        ),
    )(*args)


def row_sums(stage, data, prof):
    size = POINTS // STAGES
    points = slice(stage * size, (stage + 1) * size)
    high, low = split(data[:, points])
    part = prof[points]
    phigh, plow = split(part)
    total = dot(jnp.concatenate([high, low, high], axis=1), jnp.concatenate([phigh, phigh, plow], axis=0))
    gram = dot(phigh.T, jnp.concatenate([phigh, plow], axis=1))
    norm = jnp.broadcast_to(jnp.sum(part * part, axis=0, keepdims=True), (PAD, COMPS))
    return total, gram, norm


def early_kernel(data, prof, *sums):
    for out, value in zip(sums, row_sums(0, data, prof)):
        out[...] = value


def middle_kernel(stage, data, prof, *refs):
    for old, out, value in zip(refs[:3], refs[3:], row_sums(stage, data, prof)):
        out[...] = old[...] + value


def late_kernel(data, load, prof, total, gram_in, norm_in, send):
    more, gram, norm = row_sums(STAGES - 1, data, prof)
    gram += gram_in[...]
    mixed = gram[:, COMPS:]
    ghigh, glow = split(gram[:, :COMPS] + mixed + mixed.T)
    high, low = split(load[...])
    fitted = dot(jnp.concatenate([high, low, high], axis=1), jnp.concatenate([ghigh, ghigh, glow], axis=0))
    send[:ROWS] = total[...] + more - fitted
    send[ROWS:] = norm_in[...] + norm


SUMS = tuple(jax.ShapeDtypeStruct(shape, F32) for shape in ((ROWS, COMPS), (COMPS, 2 * COMPS), (PAD, COMPS)))
STAGES = 8


def row_part(stage, data, load, prof, sums=()):
    alias = {}
    if stage == 0:
        kernel, shapes, args = early_kernel, SUMS, (data, prof)
    elif stage < STAGES - 1:
        kernel, shapes, args = functools.partial(middle_kernel, stage), SUMS, (data, prof, *sums)
        alias = {2: 0, 3: 1, 4: 2}
    else:
        kernel, shapes = late_kernel, (jax.ShapeDtypeStruct((ROWS + PAD, COMPS), F32),)
        args = (data, load, prof, *sums)
    return pl.pallas_call(
        kernel,
        out_shape=shapes,
        in_specs=[VMEM] * len(args),
        out_specs=tuple(VMEM for _ in shapes),
        input_output_aliases=alias,
        compiler_params=pltpu.CompilerParams(vmem_limit_bytes=GRANT),
        cost_estimate=pl.CostEstimate(
            flops=6 * POINTS // STAGES * COMPS * (ROWS + COMPS),
            bytes_accessed=4 * POINTS // STAGES * (ROWS + COMPS),
            transcendentals=0,
        ),
    )(*args)


def joined_up(pieces, norms):
    add = lambda parts: functools.reduce(lambda a, b: a + b, parts)
    return jnp.concatenate([add(pieces), add(norms)], axis=0)


def updated(base, mine, other):
    rows = base.shape[0]
    grad = mine[:rows] + other[:rows]
    norm = mine[rows : rows + 1] + other[rows : rows + 1]
    return jnp.maximum(base + grad / norm, 0.0)


def load_kernel(counts, base, mine, other, out):
    grad = mine[:ROWS] + other[:ROWS]
    norm = mine[ROWS : ROWS + 1] + other[ROWS : ROWS + 1]
    fresh = jnp.maximum(base[...] + grad / norm, 0.0)
    slot = lax.broadcasted_iota(jnp.int32, fresh.shape, 0)
    out[...] = jnp.where(slot < counts[lax.axis_index("curves")], fresh, 0.0)


def load_update(counts, base, mine, other):
    return pl.pallas_call(
        load_kernel,
        out_shape=jax.ShapeDtypeStruct(base.shape, F32),
        in_specs=[pl.BlockSpec(memory_space=pltpu.SMEM), VMEM, VMEM, VMEM],
        cost_estimate=pl.CostEstimate(flops=4 * base.size, bytes_accessed=16 * base.size, transcendentals=0),
        compiler_params=pltpu.CompilerParams(vmem_limit_bytes=8 << 20),
        name="load_update",
    )(counts, base, mine, other)


def store_kernel(places, *refs):
    out, sems = refs[-2], refs[-1]
    copies = []
    for source, (colour, first, number) in zip(refs, places):
        for i in range(number):
            piece = (first + i) ^ my_piece(colour)
            start = pl.multiple_of(colour * COLOUR + piece * PIECE, PIECE)
            copies.append(
                pltpu.make_async_copy(
                    source.at[pl.ds(i * PIECE, PIECE)], out.at[pl.ds(start, PIECE)], sems.at[len(copies)]
                )
            )
    for copy in copies:
        copy.start()
    for copy in copies:
        copy.wait()


def stored(places, sources, held=None):
    args, specs, alias = list(sources), [VMEM] * len(sources), {}
    if held is not None:
        alias = {len(args): 0}
        args.append(held)
        specs.append(pl.BlockSpec(memory_space=pl.ANY))
    total = sum(number for _, _, number in places)
    return pl.pallas_call(
        functools.partial(store_kernel, places),
        out_shape=jax.ShapeDtypeStruct((POINTS, COMPS), F32),
        in_specs=specs,
        out_specs=pl.BlockSpec(memory_space=pl.ANY),
        scratch_shapes=[pltpu.SemaphoreType.DMA((total,))],
        input_output_aliases=alias,
        compiler_params=pltpu.CompilerParams(vmem_limit_bytes=8 << 20),
        cost_estimate=pl.CostEstimate(flops=0, bytes_accessed=8 * PIECE * COMPS * total, transcendentals=0),
        name="stored",
    )(*args)


def local(curves_data, loadings, profiles, counts):
    both = range(2)
    hop = lambda c, value, step: swap(value, cube_pairs(c, step))
    send, *shared = time_part("first", 0, 3, curves_data, profiles, (), counts, loadings)
    early = [hop(0, send, 0)]
    (send,) = time_part("second", 1, 3, curves_data, profiles, shared)
    early.append(hop(1, send, 0))
    (send,) = time_part("send", 0, 2, curves_data, profiles, shared)
    late = [hop(0, send, 0)]
    (send,) = time_part("send", 1, 2, curves_data, profiles, shared)
    late.append(hop(1, send, 0))
    high = time_part("keep", 0, 1, curves_data, profiles, shared)
    *low, own0, own1 = time_part("keep", 0, 0, curves_data, profiles, shared)
    owns = [own0, own1]
    sums = ()
    for stage in range(STAGES):
        sums = row_part(stage, curves_data, loadings, profiles, sums)
    row_mine = sums[0]
    row_other = swap(row_mine, CORE_PAIRS)
    row_mine = jnp.add(row_mine, row_other)
    row_far = swap(row_mine, HI_PAIRS)
    new_loadings = load_update(counts, loadings, row_mine, row_far)

    norms = [[shared[2 + c], early[c][-PAD:]] for c in both]
    one, zero = slice(PIECE, 2 * PIECE), slice(0, PIECE)
    mid = [hop(c, joined_up([high[c], early[c][:-PAD]], norms[c]), 1) for c in both]
    norms = [norms[c] + [mid[c][-PAD:]] for c in both]
    last = [hop(c, joined_up([low[c][one], late[c][one], mid[c][one]], norms[c]), 2) for c in both]
    norms = [norms[c] + [last[c][-PAD:]] for c in both]
    mine = [joined_up([m[c][zero] for m in (low, late, mid, last)], norms[c]) for c in both]
    far = [hop(c, mine[c], 3) for c in both]
    mine = [mine[c] + far[c] for c in both]
    far = [swap(mine[c], Y_PAIRS) for c in both]
    fresh = [updated(owns[c], mine[c], far[c]) for c in both]

    next1 = [hop(c, fresh[c], 2) for c in both]
    next2 = [hop(c, fresh[c], 1) for c in both]
    next4 = [hop(c, fresh[c], 0) for c in both]
    next3 = [hop(c, next1[c], 1) for c in both]
    next5 = [hop(c, next1[c], 0) for c in both]
    pair6 = hop(0, jnp.concatenate([next2[0], next3[0]], axis=0), 0)
    next6 = hop(1, next2[1], 0)
    next7 = hop(1, next3[1], 0)
    places = lambda *firsts: tuple((c, first, 1) for first in firsts for c in both)
    new_profiles = stored(places(0, 1, 2, 4, 3, 5), fresh + next1 + next2 + next4 + next3 + next5)
    new_profiles = stored(((0, 6, 2), (1, 6, 1), (1, 7, 1)), [pair6, next6, next7], new_profiles)
    return new_loadings, new_profiles


def solution(mesh):
    return jax.shard_map(
        local,
        mesh=mesh,
        in_specs=(P("curves", "tm"), P("curves", None), P("tm", None), P()),
        out_specs=(P("curves", None), P("tm", None)),
        check_vma=False,
    )
```
